32 devices in a mesh: groups: 2 (over y), attn: 4 (over x, core), expert: 4 (over z).
Axes of the slice: x: 2, y: 2, z: 4, core: 2. Of those that a mesh axis runs over, the one named last changes fastest.
Arguments:
- tokens: bfloat16 [1024, 4096], P(('groups', 'attn')), parts along dimension 0, may hold values from -6 to 6
- norm_gain: float32 [4096], replicated, may hold values from 0.1 to 1.9
- query_weight: bfloat16 [4096, 4096], P('attn', 'expert'), may hold values from -0.09375 to 0.09375
- key_weight: bfloat16 [4096, 1024], P('attn', 'expert'), may hold values from -0.09375 to 0.09375
- value_weight: bfloat16 [4096, 1024], P('attn', 'expert'), may hold values from -0.09375 to 0.09375
- out_weight: bfloat16 [4096, 4096], P('attn', 'expert'), may hold values from -0.09375 to 0.09375
- cache_key: bfloat16 [8, 2048, 1024], P(('groups', 'attn'), None, 'expert'), parts along dimension 0, may hold values from -240 to 240
- cache_value: bfloat16 [8, 2048, 1024], P(('groups', 'attn'), None, 'expert'), parts along dimension 0, may hold values from -24 to 24
- block_table: int32 [8, 8], P(('groups', 'attn')), parts along dimension 0, may hold values from 0 to 15
- block_count: int32 [8], P(('groups', 'attn')), parts along dimension 0, may hold values from 1 to 8, 24 in all
- expert_ids: int32 [1024, 2], P(('groups', 'attn')), parts along dimension 0, may hold values from 0 to 3, all different within a row; in each aligned block of 128 rows (0 to 127, 128 to 255, ...) at most 96 rows name the same one
- gate_weights: float32 [1024, 2], P(('groups', 'attn')), parts along dimension 0, may hold values from 1 to 3
- post_gain: float32 [4096], replicated, may hold values from 0.1 to 1.9
- expert_gate: bfloat16 [4, 4096, 6400], P('expert', None, 'attn'), may hold values from -0.09375 to 0.09375
- expert_up: bfloat16 [4, 4096, 6400], P('expert', None, 'attn'), may hold values from -0.09375 to 0.09375
- expert_down: bfloat16 [4, 6400, 4096], P('expert', 'attn'), may hold values from -0.15625 to 0.15625
Outputs:
- mixed: bfloat16 [1024, 4096], P(('groups', 'attn'), 'expert'), parts along dimension 0
The draws below stay inside these ranges and needn't reach their ends.
There are 2 independent parts, one for each index of `groups`. The reference program is written for one: setup_inputs(seed, part) draws one part's arguments, and reference() takes and returns one part's arrays. A program takes and returns all parts, laid end to end along the dimension named above; an argument that names none is the same for every part. Nothing has to cross between parts.
Inputs may be any that keep to these rules, and one draw needn't show every extreme that they name: `expert_ids`: in each aligned block of 128 tokens (one sequence) no expert is named more than 96 times; the two ids of a token differ. `block_count`: the counts of one part sum to 24.
All inputs are finite; a program needn't handle non-finite values. No bound on the sum of `block_count` on one device may be relied on, other than what follows from the above.
Results may differ from the reference program's by a relative error of at most 0.02.
Values may be sent and summed in bfloat16 or wider, within the bound.
No kernel may reach another device: no remote copies, remote signals or barrier semaphores. Data moves between devices by JAX's collectives and lax.ppermute only.
A program may use at most 128 MiB of HBM per device.

```python
import math
from functools import partial
import jax
import jax.numpy as jnp
import numpy as np
from jax import lax

D = 4096
HEADS = 32
KVH = 8
HD = 128
FF = 6400
ROWS = 128
CACHE_BLOCKS = 16
NSEL = 8
BLK = 128
EXPERTS = 4
SEQS = 4
TOKENS = 512
CAP = 96
N_ATTN = 4


def draw_cache_key(key, part):
    full_shape = (SEQS, CACHE_BLOCKS, BLK, KVH, HD)
    base_values = jnp.clip(jax.random.normal(jax.random.fold_in(key, 17), full_shape, jnp.float32), -6.0, 6.0)
    return base_values.reshape(SEQS, CACHE_BLOCKS * BLK, KVH * HD).astype(jnp.bfloat16)


def plant(drawn, key, least, high):
    shape = drawn.shape
    spot = [jax.random.randint(jax.random.fold_in(key, axis), (), 0, shape[axis]) for axis in range(len(shape))]
    drawn = drawn.at[tuple(spot)].set(least)
    longest = shape.index(max(shape))
    spot[longest] = (spot[longest] + 1) % shape[longest]
    return drawn.at[tuple(spot)].set(high)


def steps_of(stream_key, extent, pieces, least, high):
    def one(dim, shards_of):
        heights = jax.random.uniform(jax.random.fold_in(jax.random.fold_in(stream_key, 6), dim), (shards_of,), jnp.float32, least / len(pieces), high / len(pieces))
        return jnp.repeat(jnp.exp(heights), extent[dim] // shards_of).reshape((-1,) + (1,) * (len(extent) - dim - 1))

    gain = one(*pieces[0])
    for cut in pieces[1:]:
        gain = gain * one(*cut)
    return gain


def split_up(number_of, total, most, lean):
    portions = [(1 << 20) // math.isqrt(standing ** lean) + 1 for standing in range(2, number_of + 1)]
    spare, given = total - most - (number_of - 1), [1] * (number_of - 1)
    while spare > 0:
        movable = [i for i in range(number_of - 1) if given[i] < most]
        pool, remaining = sum([portions[i] for i in movable]), spare
        for i in movable:
            addition = min(most - given[i], max(1, remaining * portions[i] // pool), spare)
            given[i] = given[i] + addition
            spare = spare - addition
    return np.array([most] + given)


def uneven_parts(stream_key, number_of, total, limit, lean):
    if number_of == 2:
        one = jax.random.randint(stream_key, (), max(1, total - limit), min(limit, total - 1) + 1)
        return jnp.stack([one, total - one])
    sizes = jnp.asarray(split_up(number_of, total, limit, lean), jnp.int32)
    twos = (number_of - 1) // 2
    giver, sink = sizes[1:1 + 2 * twos:2], sizes[2:2 + 2 * twos:2]
    slack = jnp.minimum(giver - 1, limit - sink)
    shifted = jax.random.randint(jax.random.fold_in(stream_key, 1), (twos,), 0, 1 << 20) % (slack + 1)
    sizes = sizes.at[1:1 + 2 * twos:2].set(giver - shifted).at[2:2 + 2 * twos:2].set(sink + shifted)
    return sizes[jax.random.permutation(jax.random.fold_in(stream_key, 2), number_of)]


def shared_out(stream_key, own, number, rows, number_of, top, limit, lean):
    order = jax.random.permutation(stream_key, number_of)
    crowded, ordinary = load_shares(number_of, rows * top, limit, lean, True), load_shares(number_of, rows * top, limit, lean, False)
    places = jnp.arange(number_of)

    def named(lengths, turn):
        used = int((lengths > 0).sum())
        fixed = max(1, used // 4)
        passed = fixed + (places - fixed + turn * (used - fixed)) % max(1, number_of - fixed)
        return jnp.zeros((number_of,), jnp.int32).at[order[jnp.where(places < fixed, places, passed)]].set(jnp.asarray(lengths, jnp.int32))

    lengths = jnp.where(number % 4 == 0, named(crowded, number // 4), named(ordinary, number - number // 4 - 1))
    mixed = jax.random.permutation(jax.random.fold_in(own, 3), number_of)
    donor, receiver = mixed[0:number_of // 2 * 2:2], mixed[1:number_of // 2 * 2:2]
    slack = jnp.minimum(lengths[donor] - 1, limit - lengths[receiver]) // 2
    slack = jnp.where((donor == order[0]) | (receiver == order[0]) | (lengths[receiver] == 0), 0, jnp.maximum(slack, 0))
    passed = jax.random.randint(jax.random.fold_in(own, 4), (number_of // 2,), 0, 1 << 20) % (slack + 1)
    lengths = lengths.at[donor].add(-passed).at[receiver].add(passed)
    labels = jnp.searchsorted(jnp.cumsum(lengths), jnp.arange(rows * top), side="right").astype(jnp.int32)
    table = labels.reshape(top, rows).T
    table = table[jax.random.permutation(jax.random.fold_in(own, 1), rows)]
    turn = jax.random.randint(jax.random.fold_in(own, 2), (rows, 1), 0, top)
    return jnp.take_along_axis(table, (jnp.arange(top)[None, :] + turn) % top, axis=1)


def load_shares(amount, total, most, slope, full):
    portions = [(1 << 20) // math.isqrt(rank ** slope) + 1 for rank in range(1, amount + 1)]
    largest = most if full else min(most, max(-(-total // amount), total * portions[0] // sum(portions)))
    least = 1 if total - largest >= amount - 1 else 0
    counts, rest = [largest] + [least] * (amount - 1), total - largest - least * (amount - 1)
    while rest > 0:
        free = [i for i in range(1, amount) if counts[i] < largest] or [i for i in range(1, amount) if counts[i] < most]
        mass, remaining = sum([portions[i] for i in free]), rest
        for i in free:
            addition = min(most - counts[i], max(1, remaining * portions[i] // mass), rest)
            counts[i] = counts[i] + addition
            rest = rest - addition
    return np.array(counts)


def scatter_about(rng, shape, scale, reach, shards=(), kind=jnp.bfloat16):
    array = scale * jax.random.normal(rng, shape, jnp.float32)
    if shards:
        array = array * steps_of(rng, shape, shards, -0.22, 0.18)
    return jnp.clip(array, -reach, reach).astype(kind)


def setup_inputs(seed: int = 0, part: int = 0) -> dict:
    arg_keys = jax.random.split(jax.random.key(seed), 17)
    own_keys = jax.random.split(jax.random.fold_in(arg_keys[16], part), 17)
    tokens = scatter_about(own_keys[0], (TOKENS, D), 1.0, 6.0, ((0, 4),))
    norm_gain = jnp.clip(1.0 + 0.18 * jax.random.normal(arg_keys[1], (D,), jnp.float32), 0.1, 1.9)
    query_weight = scatter_about(arg_keys[2], (D, HEADS * HD), D ** -0.5, 0.09375, ((0, 4), (1, 4)))
    key_weight = scatter_about(arg_keys[3], (D, KVH * HD), D ** -0.5, 0.09375, ((0, 4), (1, 4)))
    value_weight = scatter_about(arg_keys[4], (D, KVH * HD), D ** -0.5, 0.09375, ((0, 4), (1, 4)))
    out_weight = scatter_about(arg_keys[5], (D, HEADS * HD), (HEADS * HD) ** -0.5, 0.09375, ((0, 4), (1, 4)))
    cache_key = draw_cache_key(jax.random.fold_in(jax.random.fold_in(arg_keys[16], part), 71), part)
    cache_value = scatter_about(own_keys[7], (SEQS, CACHE_BLOCKS * BLK, KVH * HD), 4.0, 24.0, ((0, 4), (2, 4)))
    block_table = plant(jax.random.randint(own_keys[8], (SEQS, NSEL), 0, CACHE_BLOCKS), jax.random.fold_in(own_keys[8], 1), 0, CACHE_BLOCKS - 1).astype(jnp.int32)
    block_count = uneven_parts(own_keys[9], SEQS, N_ATTN * NSEL * 3 // 4, NSEL, 2).astype(jnp.int32)
    expert_ids_keys = jax.random.split(jax.random.fold_in(own_keys[10], 1), TOKENS // ROWS)
    expert_ids_turns = jax.random.permutation(jax.random.fold_in(own_keys[10], 3), TOKENS // ROWS)
    expert_ids = jax.vmap(lambda own, number: shared_out(jax.random.fold_in(own_keys[10], 2), own, number, ROWS, EXPERTS, 2, CAP, 2))(expert_ids_keys, expert_ids_turns).reshape((TOKENS, 2))
    gate_weights = jnp.clip(1.0 + 2.0 * jax.random.uniform(own_keys[11], (TOKENS, 2), jnp.float32) ** steps_of(own_keys[11], (TOKENS, 2), ((0, 4),), -0.2, 0.2), 1.0, 3.0)
    post_gain = jnp.clip(1.0 + 0.18 * jax.random.normal(arg_keys[12], (D,), jnp.float32), 0.1, 1.9)
    expert_gate = scatter_about(arg_keys[13], (EXPERTS, D, FF), D ** -0.5, 0.09375, ((0, 4), (2, 4)))
    expert_up = scatter_about(arg_keys[14], (EXPERTS, D, FF), D ** -0.5, 0.09375, ((0, 4), (2, 4)))
    expert_down = scatter_about(arg_keys[15], (EXPERTS, FF, D), (FF // 4) ** -0.5, 0.15625, ((0, 4), (1, 4)))
    return {"tokens": tokens, "norm_gain": norm_gain, "query_weight": query_weight, "key_weight": key_weight, "value_weight": value_weight, "out_weight": out_weight, "cache_key": cache_key, "cache_value": cache_value, "block_table": block_table, "block_count": block_count, "expert_ids": expert_ids, "gate_weights": gate_weights, "post_gain": post_gain, "expert_gate": expert_gate, "expert_up": expert_up, "expert_down": expert_down}


epsilon = 1e-05
rope_base = 10000.0

def layer_norm(values, gain_vector):
    center = lax.optimization_barrier(jnp.mean(values, axis=-1, keepdims=True))
    spread = lax.optimization_barrier(jnp.mean(jnp.square(values - center), axis=-1, keepdims=True))
    return (values - center) * lax.rsqrt(spread + epsilon) * gain_vector

def rotate(values, positions, head_size):
    row_count = values.shape[0]
    head_count = values.shape[1] // head_size
    half_size = head_size // 2
    frequency = jnp.exp(jnp.arange(half_size, dtype=jnp.float32) * (-2.0 * math.log(rope_base) / head_size))
    angle_table = positions[:, None] * frequency[None, :]
    cosine = jnp.cos(angle_table)[:, None, :]
    sine_part = jnp.sin(angle_table)[:, None, :]
    split_heads = values.reshape(row_count, head_count, head_size)
    first_half = split_heads[..., :half_size]
    second_half = split_heads[..., half_size:]
    turned = jnp.concatenate([first_half * cosine - second_half * sine_part, second_half * cosine + first_half * sine_part], axis=-1)
    return turned.reshape(row_count, head_count * head_size)

def pair_slots(expert_ids, expert_total):
    flat_ids = expert_ids.reshape(-1)
    onehot = (flat_ids[:, None] == jnp.arange(expert_total, dtype=jnp.int32)[None, :]).astype(jnp.int32)
    earlier = jnp.cumsum(onehot, axis=0) - onehot
    return lax.optimization_barrier(jnp.sum(onehot * earlier, axis=1)).reshape(expert_ids.shape)

def attend(inputs):
    query_rows, fresh_keys, fresh_values, cache_keys, cache_values, block_list, live_blocks = inputs
    row_count = query_rows.shape[0]
    key_heads = fresh_keys.shape[1] // HD
    group_size = query_rows.shape[1] // fresh_keys.shape[1]
    picked_keys = jnp.take(cache_keys.reshape(CACHE_BLOCKS, BLK, -1), block_list, axis=0).reshape(NSEL * BLK, key_heads, HD)
    picked_values = jnp.take(cache_values.reshape(CACHE_BLOCKS, BLK, -1), block_list, axis=0).reshape(NSEL * BLK, key_heads, HD)
    all_keys = jnp.concatenate([picked_keys, fresh_keys.reshape(row_count, key_heads, HD)], axis=0).astype(jnp.float32)
    all_values = jnp.concatenate([picked_values, fresh_values.reshape(row_count, key_heads, HD)], axis=0).astype(jnp.float32)
    queries = query_rows.reshape(row_count, key_heads, group_size, HD).astype(jnp.float32)
    score_scale = 1.0 / math.sqrt(HD)
    scores = jnp.einsum('rkgd,nkd->kgrn', queries, all_keys) * score_scale
    live_keys = jnp.arange(NSEL * BLK, dtype=jnp.int32) // BLK < live_blocks
    row_range = jnp.arange(row_count, dtype=jnp.int32)
    causal = row_range[:, None] >= row_range[None, :]
    allowed = jnp.concatenate([jnp.broadcast_to(live_keys[None, :], (row_count, NSEL * BLK)), causal], axis=1)
    scores = jnp.where(allowed, scores, -jnp.inf)
    largest = lax.optimization_barrier(jnp.max(scores, axis=-1, keepdims=True))
    exponent = jnp.exp(scores - largest)
    weights = (exponent / lax.optimization_barrier(jnp.sum(exponent, axis=-1, keepdims=True))).astype(jnp.bfloat16)
    context = jnp.einsum('kgrn,nkd->rkgd', weights.astype(jnp.float32), all_values)
    return context.reshape(row_count, -1).astype(jnp.bfloat16)

def reference(tokens, norm_gain, query_weight, key_weight, value_weight, out_weight, cache_key, cache_value, block_table, block_count, expert_ids, gate_weights, post_gain, expert_gate, expert_up, expert_down):
    normed = layer_norm(tokens.astype(jnp.float32), norm_gain).astype(jnp.bfloat16)
    normed_wide = normed.astype(jnp.float32)
    row_range = jnp.arange(ROWS, dtype=jnp.int32)
    positions = (block_count[:, None] * BLK + row_range[None, :]).reshape(-1).astype(jnp.float32)
    query = rotate(jnp.dot(normed_wide, query_weight.astype(jnp.float32), preferred_element_type=jnp.float32), positions, HD).astype(jnp.bfloat16)
    key_new = rotate(jnp.dot(normed_wide, key_weight.astype(jnp.float32), preferred_element_type=jnp.float32), positions, HD).astype(jnp.bfloat16)
    value_new = jnp.dot(normed_wide, value_weight.astype(jnp.float32), preferred_element_type=jnp.float32).astype(jnp.bfloat16)
    context = lax.map(attend, (query.reshape(SEQS, ROWS, -1), key_new.reshape(SEQS, ROWS, -1), value_new.reshape(SEQS, ROWS, -1), cache_key, cache_value, block_table, block_count))
    context = context.reshape(TOKENS, -1)
    attended = jnp.dot(context.astype(jnp.float32), out_weight.astype(jnp.float32).T, preferred_element_type=jnp.float32)
    state = (tokens.astype(jnp.float32) + attended).astype(jnp.bfloat16)
    post_normed = layer_norm(state.astype(jnp.float32), post_gain).astype(jnp.bfloat16)
    slots = jax.vmap(partial(pair_slots, expert_total=EXPERTS))(expert_ids.reshape(SEQS, ROWS, 2)).reshape(TOKENS, 2)
    sequence_of = jnp.arange(TOKENS, dtype=jnp.int32) // ROWS
    mixture = jnp.zeros((TOKENS, D), jnp.float32)
    unit_group = FF // N_ATTN
    for expert in range(EXPERTS):
        target = jnp.where(expert_ids == expert, sequence_of[:, None] * CAP + slots, SEQS * CAP).astype(jnp.int32)
        buffer = jnp.zeros((SEQS * CAP, D), jnp.bfloat16)
        for pick in range(2):
            buffer = buffer.at[target[:, pick]].set(post_normed, mode='drop')
        buffer_wide = buffer.astype(jnp.float32)
        gated = jnp.dot(buffer_wide, expert_gate[expert].astype(jnp.float32), preferred_element_type=jnp.float32)
        lifted = jnp.dot(buffer_wide, expert_up[expert].astype(jnp.float32), preferred_element_type=jnp.float32)
        activated = lax.optimization_barrier((jax.nn.silu(gated) * lifted).astype(jnp.bfloat16)).astype(jnp.float32)
        down_wide = expert_down[expert].astype(jnp.float32)
        summed = jnp.zeros((SEQS * CAP, D), jnp.float32)
        for group_index in range(N_ATTN):
            lower = group_index * unit_group
            partial_out = jnp.dot(activated[:, lower:lower + unit_group], down_wide[lower:lower + unit_group], preferred_element_type=jnp.float32)
            summed = summed + lax.optimization_barrier(partial_out.astype(jnp.bfloat16)).astype(jnp.float32)
        expert_out = lax.optimization_barrier(summed.astype(jnp.bfloat16)).astype(jnp.float32)
        for pick in range(2):
            gathered = jnp.take(expert_out, jnp.minimum(target[:, pick], SEQS * CAP - 1), axis=0)
            chosen = (expert_ids[:, pick] == expert).astype(jnp.float32)
            mixture = mixture + gathered * (chosen * gate_weights[:, pick])[:, None]
    return (state.astype(jnp.float32) + mixture).astype(jnp.bfloat16)
```

```python
import math

import jax
import jax.numpy as jnp
from jax import lax
from jax.sharding import PartitionSpec as P

HD = 128
CACHE_BLOCKS = 16
NSEL = 8
BLK = 128


epsilon = 1e-05
rope_base = 10000.0
F32 = jnp.float32
BF16 = jnp.bfloat16


def row_statistics(values):
    center = jnp.mean(values, axis=-1, keepdims=True)
    spread = jnp.mean(jnp.square(values - center), axis=-1, keepdims=True)
    return center, lax.rsqrt(spread + epsilon)


def rotate(values, positions, head_size):
    row_count = values.shape[0]
    head_count = values.shape[1] // head_size
    half_size = head_size // 2
    frequency = jnp.exp(
        jnp.arange(half_size, dtype=jnp.float32) * (-2.0 * math.log(rope_base) / head_size)
    )
    angle_table = positions[:, None] * frequency[None, :]
    cosine = jnp.cos(angle_table)[:, None, :]
    sine_part = jnp.sin(angle_table)[:, None, :]
    split_heads = values.reshape(row_count, head_count, head_size)
    first_half = split_heads[..., :half_size]
    second_half = split_heads[..., half_size:]
    turned = jnp.concatenate(
        [
            first_half * cosine - second_half * sine_part,
            second_half * cosine + first_half * sine_part,
        ],
        axis=-1,
    )
    return turned.reshape(row_count, head_count * head_size)


def pair_slots(expert_ids, expert_total):
    flat_ids = expert_ids.reshape(-1)
    onehot = (flat_ids[:, None] == jnp.arange(expert_total, dtype=jnp.int32)[None, :]).astype(
        jnp.int32
    )
    earlier = jnp.cumsum(onehot, axis=0) - onehot
    return jnp.sum(onehot * earlier, axis=1).reshape(expert_ids.shape)


def swap(value, axis, distance):
    size = lax.axis_size(axis)
    return lax.ppermute(value, axis, [(i, i ^ distance) for i in range(size)])


def unxor(pieces, index):
    count = len(pieces)
    bit = 1
    while bit < count:
        chosen = (index & bit) != 0
        pieces = [jnp.where(chosen, pieces[k ^ bit], pieces[k]) for k in range(count)]
        bit *= 2
    return pieces


def attention(query, key_new, value_new, cache_key, cache_value, block_table, live_blocks):
    row_count, query_columns = query.shape
    key_columns = key_new.shape[1]
    row_range = jnp.arange(row_count, dtype=jnp.int32)
    key_heads = key_columns // HD
    group_size = query_columns // key_columns
    score_scale = 1.0 / math.sqrt(HD)
    queries = query.reshape(row_count, key_heads, group_size, HD)
    fresh_keys = key_new.reshape(row_count, key_heads, HD)
    fresh_values = value_new.reshape(row_count, key_heads, HD)
    causal = row_range[:, None] >= row_range[None, :]
    fresh_scores = jnp.where(
        causal,
        jnp.einsum("rkgd,nkd->kgrn", queries, fresh_keys, preferred_element_type=F32) * score_scale,
        -jnp.inf,
    )
    picked_keys = jnp.take(cache_key.reshape(CACHE_BLOCKS, BLK, key_columns), block_table, axis=0)
    picked_values = jnp.take(
        cache_value.reshape(CACHE_BLOCKS, BLK, key_columns), block_table, axis=0
    )
    flat_keys = picked_keys.reshape(NSEL * BLK, key_heads, HD)
    flat_values = picked_values.reshape(NSEL * BLK, key_heads, HD)
    live_keys = jnp.arange(NSEL * BLK, dtype=jnp.int32) // BLK < live_blocks
    cache_scores = jnp.where(
        live_keys,
        jnp.einsum("rkgd,nkd->kgrn", queries, flat_keys, preferred_element_type=F32) * score_scale,
        -jnp.inf,
    )
    largest = jnp.maximum(
        jnp.max(cache_scores, axis=-1, keepdims=True), jnp.max(fresh_scores, axis=-1, keepdims=True)
    )
    cache_exp = jnp.exp(cache_scores - largest)
    fresh_exp = jnp.exp(fresh_scores - largest)
    denominator = jnp.sum(cache_exp, axis=-1, keepdims=True) + jnp.sum(
        fresh_exp, axis=-1, keepdims=True
    )
    context = jnp.einsum(
        "kgrn,nkd->rkgd",
        (cache_exp / denominator).astype(BF16),
        flat_values,
        preferred_element_type=F32,
    )
    context = context + jnp.einsum(
        "kgrn,nkd->rkgd",
        (fresh_exp / denominator).astype(BF16),
        fresh_values,
        preferred_element_type=F32,
    )
    return context.reshape(row_count, query_columns).astype(BF16)


def shards(
    tokens,
    norm_gain,
    query_weight,
    key_weight,
    value_weight,
    out_weight,
    cache_key,
    cache_value,
    block_table,
    block_count,
    expert_ids,
    gate_weights,
    post_gain,
    expert_gate,
    expert_up,
    expert_down,
):
    seqs = lax.axis_size("attn")
    layers = lax.axis_size("expert")
    a = lax.axis_index("attn")
    e = lax.axis_index("expert")
    rows, width = tokens.shape
    block = width // seqs
    share = width // layers
    part = rows // layers
    expert_total = layers * expert_gate.shape[0]
    capacity = 3 * rows // expert_total
    query_columns = query_weight.shape[1]
    key_columns = key_weight.shape[1]

    far_first = [k for k in range(2, seqs)] + [1]
    raw = {0: lax.dynamic_slice_in_dim(tokens, a * block, block, 1)}
    for k in far_first:
        raw[k] = swap(lax.dynamic_slice_in_dim(tokens, (a ^ k) * block, block, 1), "attn", k)
    slots = pair_slots(expert_ids, expert_total)
    names = jnp.concatenate([expert_ids.T, slots.T], axis=0)
    named = {0: names}
    center, scale = row_statistics(tokens.astype(F32))
    own_stats = jnp.concatenate([center.T, scale.T], axis=0)
    stats = {0: own_stats}
    for k in far_first:
        stats[k] = swap(own_stats, "attn", k)
    for k in far_first:
        named[k] = swap(names, "attn", k)

    gain_block = lax.dynamic_slice_in_dim(norm_gain, a * block, block, 0)
    stacked = jnp.concatenate([query_weight, key_weight, value_weight], axis=1)

    def normed(k):
        center = stats[k][0][:, None]
        scale = stats[k][1][:, None]
        return ((raw[k].astype(F32) - center) * scale * gain_block).astype(BF16)

    product = {}
    for k in range(0, seqs, 2):
        both = jnp.dot(
            jnp.concatenate([normed(k), normed(k + 1)], axis=0), stacked, preferred_element_type=F32
        )
        product[k] = both[:rows]
        product[k + 1] = both[rows:].astype(BF16)
    paired = {}
    for k in list(range(2, seqs, 2)) + [0]:
        paired[k] = product[k] + swap(product[k + 1], "attn", 1).astype(F32)
    projected = paired[0]
    for k in range(2, seqs, 2):
        projected = projected + swap(paired[k].astype(BF16), "attn", k).astype(F32)

    live_blocks = block_count[0]
    row_range = jnp.arange(rows, dtype=jnp.int32)
    positions = (live_blocks * BLK + row_range).astype(F32)
    query = rotate(projected[:, :query_columns], positions, HD).astype(BF16)
    key_new = rotate(
        projected[:, query_columns : query_columns + key_columns], positions, HD
    ).astype(BF16)
    value_new = projected[:, query_columns + key_columns :].astype(BF16)
    context = attention(
        query, key_new, value_new, cache_key[0], cache_value[0], block_table[0], live_blocks
    )

    contexts = {0: context}
    for k in range(2, seqs, 2):
        contexts[k] = swap(context, "attn", k)
    for k in range(0, seqs, 2):
        contexts[k + 1] = swap(contexts[k], "attn", 1)
    state_parts = []
    for k in range(0, seqs, 2):
        partial = lax.dot_general(
            jnp.concatenate([contexts[k], contexts[k + 1]], axis=0),
            out_weight,
            (((1,), (1,)), ((), ())),
            preferred_element_type=F32,
        )
        partial = partial.astype(BF16).reshape(2, layers, part, block)
        total = lax.dynamic_index_in_dim(partial, e, 1, keepdims=False).astype(F32)
        for m in range(layers - 1, 0, -1):
            total = total + swap(
                lax.dynamic_index_in_dim(partial, e ^ m, 1, keepdims=False), "expert", m
            ).astype(F32)
        own_rows = [
            lax.dynamic_slice_in_dim(raw[j], e * part, part, 0).astype(F32) for j in (k, k + 1)
        ]
        state_parts.append((jnp.stack(own_rows) + total).astype(BF16))
    state_block = jnp.concatenate(state_parts, axis=0)

    if seqs * layers <= 16:
        pieces = {}
        for m in range(layers):
            pieces[0, m] = state_block if m == 0 else swap(state_block, "expert", m)
        for m in range(layers):
            for k in range(2, seqs, 2):
                pieces[k, m] = swap(pieces[0, m], "attn", k)
            for k in range(0, seqs, 2):
                pieces[k + 1, m] = swap(pieces[k, m], "attn", 1)

        def sequence_rows(j):
            columns = [
                jnp.concatenate([pieces[k, m][j ^ k] for m in range(layers)], axis=0)
                for k in range(seqs)
            ]
            return jnp.concatenate(unxor(columns, a), axis=1)

    else:
        in_place = jnp.stack(unxor([state_block[k] for k in range(seqs)], a))
        wide = lax.all_gather(in_place, "attn", axis=2, tiled=True)
        everything = lax.all_gather(wide, "expert", axis=1, tiled=True)

        def sequence_rows(j):
            mine = lax.dynamic_index_in_dim(everything, a ^ j, 0, keepdims=False)
            parts = [mine[m * part : (m + 1) * part] for m in range(layers)]
            return jnp.concatenate(unxor(parts, e), axis=0)

    slot_range = jnp.arange(capacity, dtype=jnp.int32)
    buffers = []
    own_state = None
    for j in range(seqs):
        gathered = sequence_rows(j)
        if j == 0:
            own_state = gathered
        name_blocks = named[j].reshape(4, layers, part)
        ordered = jnp.concatenate(
            [lax.dynamic_index_in_dim(name_blocks, e ^ m, 1, keepdims=False) for m in range(layers)],
            axis=1,
        )
        chosen = [
            (ordered[pick] == e)[None, :] & (slot_range[:, None] == ordered[2 + pick][None, :])
            for pick in range(2)
        ]
        dispatch = (chosen[0] | chosen[1]).astype(BF16)
        buffers.append(jnp.dot(dispatch, gathered, preferred_element_type=F32))
    slotted = jnp.concatenate(buffers, axis=0)
    center, scale = row_statistics(slotted)
    piece = ((slotted - center) * scale * post_gain).astype(BF16)

    gated = jnp.dot(piece, expert_gate[0], preferred_element_type=F32)
    lifted = jnp.dot(piece, expert_up[0], preferred_element_type=F32)
    activated = (jax.nn.silu(gated) * lifted).astype(BF16)
    down = expert_down[0]
    results = {}
    for m in range(layers - 1, -1, -1):
        chunk = jnp.dot(
            activated,
            lax.dynamic_slice_in_dim(down, (e ^ m) * share, share, 1),
            preferred_element_type=F32,
        ).reshape(seqs, capacity, share)
        near = {}
        for k in list(range(2, seqs, 2)) + [0]:
            near[k] = chunk[k] + swap(chunk[k + 1].astype(BF16), "attn", 1).astype(F32)
        out = near[0]
        for k in range(2, seqs, 2):
            out = out + swap(near[k].astype(BF16), "attn", k).astype(F32)
        out = out.astype(BF16)
        results[m] = out if m == 0 else swap(out, "expert", m)
    every = jnp.concatenate([results[m] for m in range(layers)], axis=0)
    column_expert = jnp.concatenate(
        [jnp.full((capacity,), e ^ m, dtype=jnp.int32) for m in range(layers)]
    )
    column_slot = jnp.concatenate([slot_range] * layers)
    mixture = jnp.zeros((rows, share), F32)
    for pick in range(2):
        place = (expert_ids[:, pick][:, None] == column_expert[None, :]) & (
            slots[:, pick][:, None] == column_slot[None, :]
        )
        mixture = mixture + gate_weights[:, pick : pick + 1] * jnp.dot(
            place.astype(BF16), every, preferred_element_type=F32
        )
    share_rows = lax.dynamic_slice_in_dim(own_state, e * share, share, 1)
    ordered_rows = unxor([share_rows[m * part : (m + 1) * part] for m in range(layers)], e)
    state_share = jnp.concatenate(ordered_rows, axis=0)
    return (state_share.astype(F32) + mixture).astype(BF16)


def solution(mesh):
    return jax.shard_map(
        shards,
        mesh=mesh,
        in_specs=(
            P(("groups", "attn"), None),
            P(),
            P("attn", "expert"),
            P("attn", "expert"),
            P("attn", "expert"),
            P("attn", "expert"),
            P(("groups", "attn"), None, "expert"),
            P(("groups", "attn"), None, "expert"),
            P(("groups", "attn"), None),
            P(("groups", "attn")),
            P(("groups", "attn"), None),
            P(("groups", "attn"), None),
            P(),
            P("expert", None, "attn"),
            P("expert", None, "attn"),
            P("expert", "attn", None),
        ),
        out_specs=P(("groups", "attn"), "expert"),
        check_vma=False,
    )
```

```python
import math

import jax
import jax.numpy as jnp
from jax import lax
from jax.experimental import pallas as pl
from jax.experimental.pallas import tpu as pltpu
from jax.sharding import PartitionSpec as P

HD = 128
CACHE_BLOCKS = 16
NSEL = 8
BLK = 128


epsilon = 1e-05
rope_base = 10000.0
F32 = jnp.float32
BF16 = jnp.bfloat16


def row_statistics(values):
    center = jnp.mean(values, axis=-1, keepdims=True)
    spread = jnp.mean(jnp.square(values - center), axis=-1, keepdims=True)
    return center, lax.rsqrt(spread + epsilon)


def rotate(values, positions, head_size):
    row_count = values.shape[0]
    head_count = values.shape[1] // head_size
    half_size = head_size // 2
    frequency = jnp.exp(
        jnp.arange(half_size, dtype=jnp.float32) * (-2.0 * math.log(rope_base) / head_size)
    )
    angle_table = positions[:, None] * frequency[None, :]
    cosine = jnp.cos(angle_table)[:, None, :]
    sine_part = jnp.sin(angle_table)[:, None, :]
    split_heads = values.reshape(row_count, head_count, head_size)
    first_half = split_heads[..., :half_size]
    second_half = split_heads[..., half_size:]
    turned = jnp.concatenate(
        [
            first_half * cosine - second_half * sine_part,
            second_half * cosine + first_half * sine_part,
        ],
        axis=-1,
    )
    return turned.reshape(row_count, head_count * head_size)


def pair_slots(expert_ids, expert_total):
    flat_ids = expert_ids.reshape(-1)
    onehot = (flat_ids[:, None] == jnp.arange(expert_total, dtype=jnp.int32)[None, :]).astype(
        jnp.int32
    )
    earlier = jnp.cumsum(onehot, axis=0) - onehot
    return jnp.sum(onehot * earlier, axis=1).reshape(expert_ids.shape)


def swap(value, axis, distance):
    size = lax.axis_size(axis)
    return lax.ppermute(value, axis, [(i, i ^ distance) for i in range(size)])


def unxor(pieces, index):
    count = len(pieces)
    bit = 1
    while bit < count:
        chosen = (index & bit) != 0
        pieces = [jnp.where(chosen, pieces[k ^ bit], pieces[k]) for k in range(count)]
        bit *= 2
    return pieces


def attention(query, key_new, value_new, cache_key, cache_value, block_table, live_blocks):
    row_count, query_columns = query.shape
    key_columns = key_new.shape[1]
    row_range = jnp.arange(row_count, dtype=jnp.int32)
    key_heads = key_columns // HD
    group_size = query_columns // key_columns
    score_scale = 1.0 / math.sqrt(HD)
    queries = query.reshape(row_count, key_heads, group_size, HD)
    fresh_keys = key_new.reshape(row_count, key_heads, HD)
    fresh_values = value_new.reshape(row_count, key_heads, HD)
    causal = row_range[:, None] >= row_range[None, :]
    fresh_scores = jnp.where(
        causal,
        jnp.einsum("rkgd,nkd->kgrn", queries, fresh_keys, preferred_element_type=F32) * score_scale,
        -jnp.inf,
    )
    picked_keys = jnp.take(cache_key.reshape(CACHE_BLOCKS, BLK, key_columns), block_table, axis=0)
    picked_values = jnp.take(
        cache_value.reshape(CACHE_BLOCKS, BLK, key_columns), block_table, axis=0
    )
    flat_keys = picked_keys.reshape(NSEL * BLK, key_heads, HD)
    flat_values = picked_values.reshape(NSEL * BLK, key_heads, HD)
    live_keys = jnp.arange(NSEL * BLK, dtype=jnp.int32) // BLK < live_blocks
    cache_scores = jnp.where(
        live_keys,
        jnp.einsum("rkgd,nkd->kgrn", queries, flat_keys, preferred_element_type=F32) * score_scale,
        -jnp.inf,
    )
    largest = jnp.maximum(
        jnp.max(cache_scores, axis=-1, keepdims=True), jnp.max(fresh_scores, axis=-1, keepdims=True)
    )
    cache_exp = jnp.exp(cache_scores - largest)
    fresh_exp = jnp.exp(fresh_scores - largest)
    denominator = jnp.sum(cache_exp, axis=-1, keepdims=True) + jnp.sum(
        fresh_exp, axis=-1, keepdims=True
    )
    context = jnp.einsum(
        "kgrn,nkd->rkgd",
        (cache_exp / denominator).astype(BF16),
        flat_values,
        preferred_element_type=F32,
    )
    context = context + jnp.einsum(
        "kgrn,nkd->rkgd",
        (fresh_exp / denominator).astype(BF16),
        fresh_values,
        preferred_element_type=F32,
    )
    return context.reshape(row_count, query_columns).astype(BF16)


def general_shards(
    tokens,
    norm_gain,
    query_weight,
    key_weight,
    value_weight,
    out_weight,
    cache_key,
    cache_value,
    block_table,
    block_count,
    expert_ids,
    gate_weights,
    post_gain,
    expert_gate,
    expert_up,
    expert_down,
):
    seqs = lax.axis_size("attn")
    layers = lax.axis_size("expert")
    a = lax.axis_index("attn")
    e = lax.axis_index("expert")
    rows, width = tokens.shape
    block = width // seqs
    share = width // layers
    part = rows // layers
    expert_total = layers * expert_gate.shape[0]
    capacity = 3 * rows // expert_total
    query_columns = query_weight.shape[1]
    key_columns = key_weight.shape[1]

    far_first = [k for k in range(2, seqs)] + [1]
    raw = {0: lax.dynamic_slice_in_dim(tokens, a * block, block, 1)}
    for k in far_first:
        raw[k] = swap(lax.dynamic_slice_in_dim(tokens, (a ^ k) * block, block, 1), "attn", k)
    slots = pair_slots(expert_ids, expert_total)
    names = jnp.concatenate([expert_ids.T, slots.T], axis=0)
    named = {0: names}
    center, scale = row_statistics(tokens.astype(F32))
    own_stats = jnp.concatenate([center.T, scale.T], axis=0)
    stats = {0: own_stats}
    for k in far_first:
        stats[k] = swap(own_stats, "attn", k)
    for k in far_first:
        named[k] = swap(names, "attn", k)

    gain_block = lax.dynamic_slice_in_dim(norm_gain, a * block, block, 0)
    stacked = jnp.concatenate([query_weight, key_weight, value_weight], axis=1)

    def normed(k):
        center = stats[k][0][:, None]
        scale = stats[k][1][:, None]
        return ((raw[k].astype(F32) - center) * scale * gain_block).astype(BF16)

    product = {}
    for k in range(0, seqs, 2):
        both = jnp.dot(
            jnp.concatenate([normed(k), normed(k + 1)], axis=0), stacked, preferred_element_type=F32
        )
        product[k] = both[:rows]
        product[k + 1] = both[rows:].astype(BF16)
    paired = {}
    for k in list(range(2, seqs, 2)) + [0]:
        paired[k] = product[k] + swap(product[k + 1], "attn", 1).astype(F32)
    projected = paired[0]
    for k in range(2, seqs, 2):
        projected = projected + swap(paired[k].astype(BF16), "attn", k).astype(F32)

    live_blocks = block_count[0]
    row_range = jnp.arange(rows, dtype=jnp.int32)
    positions = (live_blocks * BLK + row_range).astype(F32)
    query = rotate(projected[:, :query_columns], positions, HD).astype(BF16)
    key_new = rotate(
        projected[:, query_columns : query_columns + key_columns], positions, HD
    ).astype(BF16)
    value_new = projected[:, query_columns + key_columns :].astype(BF16)
    context = attention(
        query, key_new, value_new, cache_key[0], cache_value[0], block_table[0], live_blocks
    )

    contexts = {0: context}
    for k in range(2, seqs, 2):
        contexts[k] = swap(context, "attn", k)
    for k in range(0, seqs, 2):
        contexts[k + 1] = swap(contexts[k], "attn", 1)
    state_parts = []
    for k in range(0, seqs, 2):
        partial = lax.dot_general(
            jnp.concatenate([contexts[k], contexts[k + 1]], axis=0),
            out_weight,
            (((1,), (1,)), ((), ())),
            preferred_element_type=F32,
        )
        partial = partial.astype(BF16).reshape(2, layers, part, block)
        total = lax.dynamic_index_in_dim(partial, e, 1, keepdims=False).astype(F32)
        for m in range(layers - 1, 0, -1):
            total = total + swap(
                lax.dynamic_index_in_dim(partial, e ^ m, 1, keepdims=False), "expert", m
            ).astype(F32)
        own_rows = [
            lax.dynamic_slice_in_dim(raw[j], e * part, part, 0).astype(F32) for j in (k, k + 1)
        ]
        state_parts.append((jnp.stack(own_rows) + total).astype(BF16))
    state_block = jnp.concatenate(state_parts, axis=0)

    in_place = jnp.stack(unxor([state_block[k] for k in range(seqs)], a))
    wide = lax.all_gather(in_place, "attn", axis=2, tiled=True)
    everything = lax.all_gather(wide, "expert", axis=1, tiled=True)

    def sequence_rows(j):
        mine = lax.dynamic_index_in_dim(everything, a ^ j, 0, keepdims=False)
        parts = [mine[m * part : (m + 1) * part] for m in range(layers)]
        return jnp.concatenate(unxor(parts, e), axis=0)

    slot_range = jnp.arange(capacity, dtype=jnp.int32)
    buffers = []
    own_state = None
    for j in range(seqs):
        gathered = sequence_rows(j)
        if j == 0:
            own_state = gathered
        name_blocks = named[j].reshape(4, layers, part)
        ordered = jnp.concatenate(
            [lax.dynamic_index_in_dim(name_blocks, e ^ m, 1, keepdims=False) for m in range(layers)],
            axis=1,
        )
        chosen = [
            (ordered[pick] == e)[None, :] & (slot_range[:, None] == ordered[2 + pick][None, :])
            for pick in range(2)
        ]
        dispatch = (chosen[0] | chosen[1]).astype(BF16)
        buffers.append(jnp.dot(dispatch, gathered, preferred_element_type=F32))
    slotted = jnp.concatenate(buffers, axis=0)
    center, scale = row_statistics(slotted)
    piece = ((slotted - center) * scale * post_gain).astype(BF16)

    gated = jnp.dot(piece, expert_gate[0], preferred_element_type=F32)
    lifted = jnp.dot(piece, expert_up[0], preferred_element_type=F32)
    activated = (jax.nn.silu(gated) * lifted).astype(BF16)
    down = expert_down[0]
    results = {}
    for m in range(layers - 1, -1, -1):
        chunk = jnp.dot(
            activated,
            lax.dynamic_slice_in_dim(down, (e ^ m) * share, share, 1),
            preferred_element_type=F32,
        ).reshape(seqs, capacity, share)
        near = {}
        for k in list(range(2, seqs, 2)) + [0]:
            near[k] = chunk[k] + swap(chunk[k + 1].astype(BF16), "attn", 1).astype(F32)
        out = near[0]
        for k in range(2, seqs, 2):
            out = out + swap(near[k].astype(BF16), "attn", k).astype(F32)
        out = out.astype(BF16)
        results[m] = out if m == 0 else swap(out, "expert", m)
    every = jnp.concatenate([results[m] for m in range(layers)], axis=0)
    column_expert = jnp.concatenate(
        [jnp.full((capacity,), e ^ m, dtype=jnp.int32) for m in range(layers)]
    )
    column_slot = jnp.concatenate([slot_range] * layers)
    mixture = jnp.zeros((rows, share), F32)
    for pick in range(2):
        place = (expert_ids[:, pick][:, None] == column_expert[None, :]) & (
            slots[:, pick][:, None] == column_slot[None, :]
        )
        mixture = mixture + gate_weights[:, pick : pick + 1] * jnp.dot(
            place.astype(BF16), every, preferred_element_type=F32
        )
    share_rows = lax.dynamic_slice_in_dim(own_state, e * share, share, 1)
    ordered_rows = unxor([share_rows[m * part : (m + 1) * part] for m in range(layers)], e)
    state_share = jnp.concatenate(ordered_rows, axis=0)
    return (state_share.astype(F32) + mixture).astype(BF16)


VMEM = pl.BlockSpec(memory_space=pltpu.VMEM)
SMEM = pl.BlockSpec(memory_space=pltpu.SMEM)
HBM = pl.BlockSpec(memory_space=pl.ANY)


def prepare_body(place, tokens, gain, *refs):
    seqs = (len(refs) - 1) // 2
    blocks, raws, full = refs[:seqs], refs[seqs:-1], refs[-1]
    rows, width = tokens.shape
    block = width // seqs
    part = raws[0].shape[0]
    a, e = place[0], place[1]
    for low in range(0, rows, 32):
        values = tokens[low : low + 32, :].astype(F32)
        center = jnp.mean(values, axis=-1, keepdims=True)
        away = values - center
        scale = lax.rsqrt(jnp.mean(away * away, axis=-1, keepdims=True) + epsilon)
        full[low : low + 32, :] = (away * scale * gain[...]).astype(BF16)
    for k in range(seqs):
        columns = pl.ds(pl.multiple_of((a ^ k) * block, 128), block)
        blocks[k][...] = full[:, columns]
        raws[k][...] = tokens[pl.ds(pl.multiple_of(e * part, 16), part), columns]


def prepare(place, tokens, gain, seqs, part):
    rows, width = tokens.shape
    block = width // seqs
    shapes = [jax.ShapeDtypeStruct((rows, block), BF16)] * seqs
    shapes += [jax.ShapeDtypeStruct((part, block), BF16)] * seqs
    outs = pl.pallas_call(
        prepare_body,
        out_shape=shapes,
        in_specs=[SMEM, VMEM, VMEM],
        out_specs=[VMEM] * (2 * seqs),
        scratch_shapes=[pltpu.VMEM((rows, width), BF16)],
        name="prepare",
    )(place, tokens, gain)
    return outs[:seqs], outs[seqs:]


def project_body(even, odd, query, key, value, even_out, odd_out):
    rows = even.shape[0]
    both = jnp.concatenate([even[...], odd[...]], axis=0)
    low = 0
    for weight in (query, key, value):
        high = low + weight.shape[1]
        result = jnp.dot(both, weight[...], preferred_element_type=F32)
        even_out[:, low:high] = result[:rows]
        odd_out[:, low:high] = result[rows:].astype(BF16)
        low = high


def project(even, odd, query, key, value):
    rows = even.shape[0]
    columns = query.shape[1] + key.shape[1] + value.shape[1]
    return pl.pallas_call(
        project_body,
        out_shape=[
            jax.ShapeDtypeStruct((rows, columns), F32),
            jax.ShapeDtypeStruct((rows, columns), BF16),
        ],
        in_specs=[VMEM] * 5,
        out_specs=[VMEM] * 2,
        name="project",
    )(even, odd, query, key, value)


def attend_body(table, count, near, *refs):
    far, (cosine, sine, keys, values, out, picked_keys, picked_values) = refs[:-7], refs[-7:]
    rows, query_columns = out.shape
    key_columns = keys.shape[1]
    group = query_columns // key_columns
    listed = picked_keys.shape[0]
    live = count[0]
    for j in range(NSEL):
        source = pl.ds(pl.multiple_of(table[0, j] * BLK, BLK), BLK)
        picked_keys[j * BLK : (j + 1) * BLK, :] = keys[source, :]
        picked_values[j * BLK : (j + 1) * BLK, :] = values[source, :]

    def raw(low):
        total = near[:, low : low + HD]
        for other in far:
            total = total + other[:, low : low + HD].astype(F32)
        return total

    def turned(low):
        head = raw(low)
        return (head * cosine[...] + pltpu.roll(head, HD // 2, 1) * sine[...]).astype(BF16)

    row = lax.broadcasted_iota(jnp.int32, (rows, rows), 0)
    column = lax.broadcasted_iota(jnp.int32, (rows, rows), 1)
    causal = row >= column
    alive = lax.broadcasted_iota(jnp.int32, (rows, listed), 1) < live * BLK
    scale = 1.0 / math.sqrt(HD)
    contract = (((1,), (1,)), ((), ()))
    for g in range(key_columns // HD):
        fresh_key = turned(query_columns + g * HD)
        fresh_value = raw(query_columns + key_columns + g * HD).astype(BF16)
        old_key = picked_keys[:, g * HD : (g + 1) * HD]
        old_value = picked_values[:, g * HD : (g + 1) * HD]
        for q in range(group):
            low = (g * group + q) * HD
            query = turned(low)
            fresh = lax.dot_general(query, fresh_key, contract, preferred_element_type=F32)
            fresh = jnp.where(causal, fresh * scale, -jnp.inf)
            old = lax.dot_general(query, old_key, contract, preferred_element_type=F32)
            old = jnp.where(alive, old * scale, -jnp.inf)
            top = jnp.maximum(
                jnp.max(fresh, axis=-1, keepdims=True), jnp.max(old, axis=-1, keepdims=True)
            )
            fresh = jnp.exp(fresh - top)
            old = jnp.exp(old - top)
            total = jnp.sum(fresh, axis=-1, keepdims=True) + jnp.sum(old, axis=-1, keepdims=True)
            mixed = jnp.dot(old.astype(BF16), old_value, preferred_element_type=F32)
            mixed = mixed + jnp.dot(fresh.astype(BF16), fresh_value, preferred_element_type=F32)
            out[:, low : low + HD] = (mixed / total).astype(BF16)


def attend(table, count, near, far, cosine, sine, keys, values, query_columns):
    rows = near.shape[0]
    key_columns = keys.shape[1]
    return pl.pallas_call(
        attend_body,
        out_shape=jax.ShapeDtypeStruct((rows, query_columns), BF16),
        in_specs=[SMEM, SMEM] + [VMEM] * (5 + len(far)),
        out_specs=VMEM,
        scratch_shapes=[
            pltpu.VMEM((NSEL * BLK, key_columns), BF16),
            pltpu.VMEM((NSEL * BLK, key_columns), BF16),
        ],
        name="attend",
    )(table, count, near, *far, cosine, sine, keys, values)


def experts_body(seqs, layers, tiles, place, *refs):
    count = seqs * layers
    pieces = refs[:count]
    names, gain, gate_hbm, up_hbm, down_hbm, share_out = refs[count : count + 6]
    outs = refs[count + 6 : count + 6 + layers]
    state, slotted, hidden, gate, up, down, piece_sem, gate_sem, up_sem, down_sem = refs[
        count + 6 + layers :
    ]
    rows, width = state.shape[1:]
    capacity = slotted.shape[0] // seqs
    part = rows // layers
    block = width // seqs
    share = share_out.shape[1]
    a, e = place[0], place[1]
    moves = []
    for k in range(seqs):
        columns = pl.ds(pl.multiple_of((a ^ k) * block, 128), block)
        for m in range(layers):
            own_rows = pl.ds(pl.multiple_of((e ^ m) * part, 16), part)
            for j in range(seqs):
                move = pltpu.make_async_copy(
                    pieces[k * layers + m].at[j ^ k], state.at[j, own_rows, columns], piece_sem.at[j]
                )
                move.start()
                moves.append((j, move))
    loads = []
    for c, (low, high) in enumerate(tiles):
        span = pl.ds(low, high - low)
        pair = (
            pltpu.make_async_copy(gate_hbm.at[span, :], gate.at[span, :], gate_sem.at[c]),
            pltpu.make_async_copy(up_hbm.at[span, :], up.at[span, :], up_sem.at[c]),
        )
        pair[0].start()
        pair[1].start()
        loads.append(pair)
    lowered = []
    for n, m in enumerate(range(layers - 1, -1, -1)):
        columns = pl.ds(pl.multiple_of((e ^ m) * share, 128), share)
        load = pltpu.make_async_copy(down_hbm.at[:, columns], down.at[n], down_sem.at[n])
        load.start()
        lowered.append(load)

    slot = lax.broadcasted_iota(jnp.int32, (capacity, rows), 0)
    step = 32
    for j in range(seqs):
        for owner, move in moves:
            if owner == j:
                move.wait()
        chosen = None
        for pick in range(2):
            named = names[j, pick : pick + 1, :]
            at = names[j, 2 + pick : 3 + pick, :]
            hit = (named == e) & (at == slot)
            chosen = hit if chosen is None else chosen | hit
        dispatch = jnp.where(chosen, 1.0, 0.0).astype(BF16)
        for low in range(0, width, block):
            picked = jnp.dot(
                dispatch, state[j, :, low : low + block], preferred_element_type=F32
            )
            slotted[j * capacity : (j + 1) * capacity, low : low + block] = picked.astype(BF16)
        for low in range(j * capacity, (j + 1) * capacity, step):
            values = slotted[low : low + step, :].astype(F32)
            center = jnp.mean(values, axis=-1, keepdims=True)
            away = values - center
            scale = lax.rsqrt(jnp.mean(away * away, axis=-1, keepdims=True) + epsilon)
            slotted[low : low + step, :] = (away * scale * gain[...]).astype(BF16)
    share_out[...] = state[0, :, pl.ds(pl.multiple_of(e * share, 128), share)]

    contract = (((1,), (1,)), ((), ()))
    for c, (low, high) in enumerate(tiles):
        loads[c][0].wait()
        gated = lax.dot_general(
            slotted[...], gate[low:high, :], contract, preferred_element_type=F32
        )
        loads[c][1].wait()
        lifted = lax.dot_general(
            slotted[...], up[low:high, :], contract, preferred_element_type=F32
        )
        hidden[:, low:high] = (gated / (1.0 + jnp.exp(-gated)) * lifted).astype(BF16)
    for n in range(layers):
        lowered[n].wait()
        outs[n][...] = jnp.dot(hidden[...], down[n], preferred_element_type=F32).astype(BF16)


def experts(place, pieces, names, gain, gate, up, down, seqs, layers, rows, capacity, share):
    units, width = gate.shape
    slots = seqs * capacity
    wide = max(128, units // 4 // 128 * 128)
    edges = list(range(0, units, wide))
    if len(edges) > 1 and units - edges[-1] < wide // 2:
        edges.pop()
    tiles = list(zip(edges, edges[1:] + [units]))
    cut = len(tiles)
    return pl.pallas_call(
        lambda *refs: experts_body(seqs, layers, tiles, *refs),
        out_shape=[jax.ShapeDtypeStruct((rows, share), BF16)]
        + [jax.ShapeDtypeStruct((slots, share), BF16)] * layers,
        in_specs=[SMEM] + [HBM] * len(pieces) + [VMEM] * 2 + [HBM] * 3,
        out_specs=[VMEM] * (1 + layers),
        scratch_shapes=[
            pltpu.VMEM((seqs, rows, width), BF16),
            pltpu.VMEM((slots, width), BF16),
            pltpu.VMEM((slots, units), BF16),
            pltpu.VMEM((units, width), BF16),
            pltpu.VMEM((units, width), BF16),
            pltpu.VMEM((layers, units, share), BF16),
            pltpu.SemaphoreType.DMA((seqs,)),
            pltpu.SemaphoreType.DMA((cut,)),
            pltpu.SemaphoreType.DMA((cut,)),
            pltpu.SemaphoreType.DMA((layers,)),
        ],
        compiler_params=pltpu.CompilerParams(vmem_limit_bytes=60 * 1024 * 1024),
        name="experts",
    )(place, *pieces, names, gain, gate, up, down)


def after(value, earlier):
    return lax.optimization_barrier((value, earlier))[0]


def small_shards(
    tokens,
    norm_gain,
    query_weight,
    key_weight,
    value_weight,
    out_weight,
    cache_key,
    cache_value,
    block_table,
    block_count,
    expert_ids,
    gate_weights,
    post_gain,
    expert_gate,
    expert_up,
    expert_down,
):
    seqs = lax.axis_size("attn")
    layers = lax.axis_size("expert")
    a = lax.axis_index("attn")
    e = lax.axis_index("expert")
    place = jnp.stack([a, e]).astype(jnp.int32)
    rows, width = tokens.shape
    block = width // seqs
    share = width // layers
    part = rows // layers
    expert_total = layers * expert_gate.shape[0]
    capacity = 3 * rows // expert_total
    query_columns = query_weight.shape[1]

    sent, raw_sent = prepare(place, tokens, norm_gain[None, :], seqs, part)
    normed = {0: sent[0]}
    for k in list(range(2, seqs)) + [1]:
        normed[k] = swap(sent[k], "attn", k)
    slots = pair_slots(expert_ids, expert_total)
    names = jnp.concatenate([expert_ids.T, slots.T], axis=0)

    live_blocks = block_count[0]
    positions = (live_blocks * BLK + jnp.arange(rows, dtype=jnp.int32)).astype(F32)
    frequency = jnp.exp(
        jnp.arange(HD // 2, dtype=F32) * (-2.0 * math.log(rope_base) / HD)
    )
    angle = positions[:, None] * frequency[None, :]
    cosine = jnp.concatenate([jnp.cos(angle)] * 2, axis=1)
    sine = jnp.concatenate([-jnp.sin(angle), jnp.sin(angle)], axis=1)

    product = {}
    for k in range(0, seqs, 2):
        product[k], product[k + 1] = project(
            normed[k], normed[k + 1], query_weight, key_weight, value_weight
        )
    paired = {}
    for k in list(range(2, seqs, 2)) + [0]:
        paired[k] = product[k] + swap(product[k + 1], "attn", 1).astype(F32)
    far = [swap(paired[k].astype(BF16), "attn", k) for k in range(2, seqs, 2)]
    raw = {0: raw_sent[0]}
    named = {0: names}
    for k in range(1, seqs):
        raw[k] = swap(after(raw_sent[k], product[0]), "attn", k)
        named[k] = swap(after(names, product[0]), "attn", k)
    near, settled = lax.optimization_barrier(
        (paired[0], ([raw[k] for k in range(seqs)], [named[k] for k in range(seqs)]))
    )
    raw, named = dict(enumerate(settled[0])), dict(enumerate(settled[1]))
    context = attend(
        block_table,
        block_count,
        near,
        far,
        cosine,
        sine,
        cache_key[0],
        cache_value[0],
        query_columns,
    )

    contexts = {0: context}
    for k in range(2, seqs, 2):
        contexts[k] = swap(context, "attn", k)
    for k in range(0, seqs, 2):
        contexts[k + 1] = swap(contexts[k], "attn", 1)
    state_parts = []
    for k in range(0, seqs, 2):
        partial = lax.dot_general(
            jnp.concatenate([contexts[k], contexts[k + 1]], axis=0),
            out_weight,
            (((1,), (1,)), ((), ())),
            preferred_element_type=F32,
        )
        partial = partial.astype(BF16).reshape(2, layers, part, block)
        total = lax.dynamic_index_in_dim(partial, e, 1, keepdims=False).astype(F32)
        for m in range(layers - 1, 0, -1):
            total = total + swap(
                lax.dynamic_index_in_dim(partial, e ^ m, 1, keepdims=False), "expert", m
            ).astype(F32)
        own_rows = [raw[j].astype(F32) for j in (k, k + 1)]
        state_parts.append((jnp.stack(own_rows) + total).astype(BF16))
    state_block = jnp.concatenate(state_parts, axis=0)

    pieces = {(0, 0): state_block}
    for m in range(1, layers):
        source = state_block if m < 3 else after(state_block, pieces[0, m - 2])
        pieces[0, m] = swap(source, "expert", m)
    for m in range(layers):
        for k in range(2, seqs, 2):
            pieces[k, m] = swap(pieces[0, m], "attn", k)
        for k in range(0, seqs, 2):
            pieces[k + 1, m] = swap(pieces[k, m], "attn", 1)
    state_share, *chunks = experts(
        place,
        [pieces[k, m] for k in range(seqs) for m in range(layers)],
        jnp.stack([named[k] for k in range(seqs)]),
        post_gain[None, :],
        jnp.swapaxes(expert_gate[0], 0, 1),
        jnp.swapaxes(expert_up[0], 0, 1),
        expert_down[0],
        seqs,
        layers,
        rows,
        capacity,
        share,
    )
    results = {}
    for m in range(layers - 1, -1, -1):
        chunk = chunks[layers - 1 - m].reshape(seqs, capacity, share)
        near = {}
        for k in list(range(2, seqs, 2)) + [0]:
            near[k] = chunk[k].astype(F32) + swap(chunk[k + 1], "attn", 1).astype(F32)
        out = near[0]
        for k in range(2, seqs, 2):
            out = out + swap(near[k].astype(BF16), "attn", k).astype(F32)
        out = out.astype(BF16)
        results[m] = out if m == 0 else swap(out, "expert", m)
    every = jnp.concatenate([results[m] for m in range(layers)], axis=0)
    slot_range = jnp.arange(capacity, dtype=jnp.int32)
    column_expert = jnp.concatenate(
        [jnp.full((capacity,), e ^ m, dtype=jnp.int32) for m in range(layers)]
    )
    column_slot = jnp.concatenate([slot_range] * layers)
    mixture = jnp.zeros((rows, share), F32)
    for pick in range(2):
        spot = (expert_ids[:, pick][:, None] == column_expert[None, :]) & (
            slots[:, pick][:, None] == column_slot[None, :]
        )
        mixture = mixture + gate_weights[:, pick : pick + 1] * jnp.dot(
            spot.astype(BF16), every, preferred_element_type=F32
        )
    return (state_share.astype(F32) + mixture).astype(BF16)


def solution(mesh):
    small = mesh.shape["attn"] * mesh.shape["expert"] <= 16
    return jax.shard_map(
        small_shards if small else general_shards,
        mesh=mesh,
        in_specs=(
            P(("groups", "attn"), None),
            P(),
            P("attn", "expert"),
            P("attn", "expert"),
            P("attn", "expert"),
            P("attn", "expert"),
            P(("groups", "attn"), None, "expert"),
            P(("groups", "attn"), None, "expert"),
            P(("groups", "attn"), None),
            P(("groups", "attn")),
            P(("groups", "attn"), None),
            P(("groups", "attn"), None),
            P(),
            P("expert", None, "attn"),
            P("expert", None, "attn"),
            P("expert", "attn", None),
        ),
        out_specs=P(("groups", "attn"), "expert"),
        check_vma=False,
    )
```
